32 devices in a mesh: groups: 2 (over y), dp: 4 (over x, core), tensor: 4 (over z).
Axes of the slice: x: 2, y: 2, z: 4, core: 2. Of those that a mesh axis runs over, the one named last changes fastest.
Arguments:
- query: bfloat16 [4096, 512], P(('groups', 'dp'), 'tensor'), parts along dimension 0, may hold values from -4.5 to 4.5
- keys: bfloat16 [4096, 512], P(('groups', 'dp'), 'tensor'), parts along dimension 0, may hold values from -4.5 to 4.5
- values: bfloat16 [4096, 512], P(('groups', 'dp'), 'tensor'), parts along dimension 0, may hold values from -6 to 6
- upstream: bfloat16 [4096, 8192], P(('groups', 'dp', 'tensor')), parts along dimension 0, may hold values from -6 to 6
- projection: bfloat16 [512, 8192], P('tensor', 'dp'), may hold values from -0.0625 to 0.0625
- lengths: int32 [8, 8], P(('groups', 'dp')), parts along dimension 0, may hold values from 1 to 256, 512 in all within a row
Outputs:
- grad_query: bfloat16 [4096, 512], P(('groups', 'dp'), 'tensor'), parts along dimension 0
- grad_keys: bfloat16 [4096, 512], P(('groups', 'dp'), 'tensor'), parts along dimension 0
- grad_values: bfloat16 [4096, 512], P(('groups', 'dp'), 'tensor'), parts along dimension 0
- grad_projection: float32 [1024, 8192], P(('groups', 'tensor'), 'dp'), parts along dimension 0
The draws below stay inside these ranges and needn't reach their ends.
There are 2 independent parts, one for each index of `groups`. The reference program is written for one: setup_inputs(seed, part) draws one part's arguments, and reference() takes and returns one part's arrays. A program takes and returns all parts, laid end to end along the dimension named above; an argument that names none is the same for every part. Nothing has to cross between parts.
Inputs may be any that keep to these rules, and one draw needn't show every extreme that they name: Each row holds the lengths of the 8 documents of one sequence in order; they sum to 512 and the largest is exactly 256.
All inputs are finite; a program needn't handle non-finite values.
Results may differ from the reference program's by a relative error of at most 0.014.
Values may be sent and summed in bfloat16 or wider, within the bound.
No kernel may reach another device: no remote copies, remote signals or barrier semaphores. Data moves between devices by JAX's collectives and lax.ppermute only.
A program may use at most 64 MiB of HBM per device.

```python
import math
import jax
import jax.numpy as jnp
import numpy as np
from jax import lax

D = 8192
HD = 128
LEN = 512
SEGS = 8
HEADS = 4
SEQS = 4
TOKENS = 2048


def drawn_pair(key):
    shape = (TOKENS, HEADS * HD)
    key_query, key_keys = jax.random.split(key, 2)
    query_draw = jnp.clip(jax.random.normal(key_query, shape, jnp.float32), -4.5, 4.5)
    keys_draw = jnp.clip(jax.random.normal(key_keys, shape, jnp.float32), -4.5, 4.5)
    return (query_draw, keys_draw)


def draw_query(key, part):
    return drawn_pair(jax.random.fold_in(key, 11))[0].astype(jnp.bfloat16)


def draw_keys(key, part):
    return drawn_pair(jax.random.fold_in(key, 11))[1].astype(jnp.bfloat16)


def strengthened(values, key, source, target, parts, factor):
    owner, partner = [(jnp.arange(values.shape[position]) // (values.shape[position] // parts)).reshape([-1 if axis == position else 1 for axis in range(values.ndim)]) for position in (source, target)]
    chosen = jax.random.permutation(key, parts)[partner]
    strong = (owner == chosen) | (owner == (partner + parts // 2) % parts)
    return jnp.where(strong, factor * values, values)


def block_scale(stream_key, shape, cuts, least, top_value):
    loudness = 1.0
    for axis_at, parts in cuts:
        draws = jax.random.uniform(jax.random.fold_in(jax.random.fold_in(stream_key, 6), axis_at), (parts,), jnp.float32, least / len(cuts), top_value / len(cuts))
        loudness = loudness * jnp.repeat(jnp.exp(draws), shape[axis_at] // parts).reshape((-1,) + (1,) * (len(shape) - 1 - axis_at))
    return loudness


def split_up(number_of, total, limit, slope):
    portions = [(1 << 20) // math.isqrt(grade ** slope) + 1 for grade in range(2, number_of + 1)]
    surplus, holding = total - limit - (number_of - 1), [1] * (number_of - 1)
    while surplus > 0:
        free = [i for i in range(number_of - 1) if holding[i] < limit]
        mass, budget = sum([portions[i] for i in free]), surplus
        for i in free:
            extra = min(limit - holding[i], max(1, budget * portions[i] // mass), surplus)
            holding[i] = holding[i] + extra
            surplus = surplus - extra
    return np.array([limit] + holding)


def uneven_parts(key, amount, total, reach, skew):
    if amount == 2:
        one = jax.random.randint(key, (), max(1, total - reach), min(reach, total - 1) + 1)
        return jnp.stack([one, total - one])
    sizes = jnp.asarray(split_up(amount, total, reach, skew), jnp.int32)
    twos = (amount - 1) // 2
    source_of, sink = sizes[1:1 + 2 * twos:2], sizes[2:2 + 2 * twos:2]
    slack = jnp.minimum(source_of - 1, reach - sink)
    shifted = jax.random.randint(jax.random.fold_in(key, 1), (twos,), 0, 1 << 20) % (slack + 1)
    sizes = sizes.at[1:1 + 2 * twos:2].set(source_of - shifted).at[2:2 + 2 * twos:2].set(sink + shifted)
    return sizes[jax.random.permutation(jax.random.fold_in(key, 2), amount)]


def noise(rng, extent, scale, bound, pieces=(), kind=jnp.bfloat16):
    values = scale * jax.random.normal(rng, extent, jnp.float32)
    if pieces:
        values = values * block_scale(rng, extent, pieces, -0.22, 0.18)
    return jnp.clip(values, -bound, bound).astype(kind)


def bell_draw_with(rng, dims, scale, most, cuts, heavy, kind=jnp.bfloat16):
    result = scale * jax.random.normal(rng, dims, jnp.float32)
    if cuts:
        result = result * block_scale(rng, dims, cuts, -0.22, 0.18)
    return jnp.clip(strengthened(result, jax.random.fold_in(rng, 3), *heavy), -most, most).astype(kind)


def setup_inputs(seed: int = 0, part: int = 0) -> dict:
    arg_keys = jax.random.split(jax.random.key(seed), 7)
    own_keys = jax.random.split(jax.random.fold_in(arg_keys[6], part), 7)
    query = draw_query(jax.random.fold_in(jax.random.fold_in(arg_keys[6], part), 71), part)
    keys = draw_keys(jax.random.fold_in(jax.random.fold_in(arg_keys[6], part), 71), part)
    values = noise(own_keys[2], (TOKENS, HEADS * HD), 1.0, 6.0, ((0, 4), (1, 4)))
    upstream = bell_draw_with(own_keys[3], (TOKENS, D), 1.0, 6.0, ((0, 16),), (0, 1, 16, 2.0))
    projection = noise(arg_keys[4], (HEADS * HD, D), D ** -0.5, 0.0625, ((0, 4), (1, 4)))
    lengths = jax.vmap(lambda own: uneven_parts(own, SEGS, LEN, LEN // 2, 2))(jax.random.split(own_keys[5], SEQS)).reshape((SEQS, SEGS)).astype(jnp.int32)
    return {"query": query, "keys": keys, "values": values, "upstream": upstream, "projection": projection, "lengths": lengths}


def sequence_mask(length_row):
    segment_ends = jnp.cumsum(length_row)
    places = jnp.arange(LEN, dtype=jnp.int32)
    labels = jnp.sum((segment_ends[None, :] <= places[:, None]).astype(jnp.int32), axis=1)
    same = labels[:, None] == labels[None, :]
    return jnp.logical_and(same, places[None, :] <= places[:, None])


def reference(query, keys, values, upstream, projection, lengths):
    scaling = HD ** -0.5
    width = HEADS * HD

    def one_sequence(carry, index):
        start = (index * LEN).astype(jnp.int32)
        query_rows = lax.dynamic_slice_in_dim(query, start, LEN, 0)
        key_rows = lax.dynamic_slice_in_dim(keys, start, LEN, 0)
        value_rows = lax.dynamic_slice_in_dim(values, start, LEN, 0)
        upstream_rows = lax.dynamic_slice_in_dim(upstream, start, LEN, 0)
        length_row = lax.dynamic_index_in_dim(lengths, index, 0, keepdims=False)
        allowed = sequence_mask(length_row)
        query_heads = query_rows.reshape(LEN, HEADS, HD).astype(jnp.float32)
        key_heads = key_rows.reshape(LEN, HEADS, HD).astype(jnp.float32)
        value_heads = value_rows.reshape(LEN, HEADS, HD).astype(jnp.float32)
        scores = jnp.einsum("qhd,khd->hqk", query_heads, key_heads) * scaling
        scores = jnp.where(allowed[None], scores, -1e30)
        row_max = jnp.max(scores, axis=2, keepdims=True)
        exponent = jnp.exp(scores - row_max)
        probs = exponent / jnp.sum(exponent, axis=2, keepdims=True)
        probs_low = probs.astype(jnp.bfloat16)
        attended = jnp.einsum("hqk,khd->qhd", probs_low.astype(jnp.float32), value_heads)
        attended = attended.astype(jnp.bfloat16).reshape(LEN, width)
        out_grad = jnp.dot(upstream_rows, projection.T, preferred_element_type=jnp.float32).astype(jnp.bfloat16)
        partial_grad = jnp.dot(attended.T, upstream_rows, preferred_element_type=jnp.float32)
        grad_heads = out_grad.reshape(LEN, HEADS, HD).astype(jnp.float32)
        grad_values = jnp.einsum("hqk,qhd->khd", probs_low.astype(jnp.float32), grad_heads).astype(jnp.bfloat16)
        grad_probs = jnp.einsum("qhd,khd->hqk", grad_heads, value_heads)
        delta = jnp.sum(probs * grad_probs, axis=2, keepdims=True)
        grad_scores = (probs * (grad_probs - delta) * scaling).astype(jnp.bfloat16).astype(jnp.float32)
        grad_query = jnp.einsum("hqk,khd->qhd", grad_scores, key_heads).astype(jnp.bfloat16)
        grad_keys = jnp.einsum("hqk,qhd->khd", grad_scores, query_heads).astype(jnp.bfloat16)
        outputs = (grad_query.reshape(LEN, width), grad_keys.reshape(LEN, width), grad_values.reshape(LEN, width))
        return carry + partial_grad, outputs

    initial = jnp.zeros((width, D), jnp.float32)
    indices = jnp.arange(SEQS, dtype=jnp.int32)
    grad_projection, stacked = lax.scan(one_sequence, initial, indices)
    grad_query = stacked[0].reshape(TOKENS, width)
    grad_keys = stacked[1].reshape(TOKENS, width)
    grad_values = stacked[2].reshape(TOKENS, width)
    return grad_query, grad_keys, grad_values, grad_projection
```

```python
import jax
import jax.numpy as jnp
from jax import lax
from jax.sharding import PartitionSpec as P

HD = 128
CHUNKS = 2


def sequence_mask(length_row, row_count):
    segment_ends = jnp.cumsum(length_row)
    places = jnp.arange(row_count, dtype=jnp.int32)
    labels = jnp.sum((segment_ends[None, :] <= places[:, None]).astype(jnp.int32), axis=1)
    same = labels[:, None] == labels[None, :]
    return jnp.logical_and(same, places[None, :] <= places[:, None])


def dot(a, b, contract):
    return lax.dot_general(a, b, ((contract[0], contract[1]), ((), ())), preferred_element_type=jnp.float32)


def build(dp, tensor):
    spans = dp // 2
    bf = jnp.bfloat16

    def core_swap(value):
        return lax.ppermute(value, "dp", [(i, i ^ 1) for i in range(dp)])

    def span_shift(value, step):
        perm = [(i, ((i // 2 + step) % spans) * 2 + i % 2) for i in range(dp)]
        return lax.ppermute(value, "dp", perm)

    def ring_shift(value, step):
        return lax.ppermute(value, "tensor", [(i, (i + step) % tensor) for i in range(tensor)])

    def up(value, first, last):
        return lax.ppermute(value, "tensor", [(i, i + 1) for i in range(first, last)])

    def down(value, first, last):
        return lax.ppermute(value, "tensor", [(i, i - 1) for i in range(first, last)])

    def shards(query, keys, values, upstream, projection, lengths):
        rows = query.shape[0]
        part = upstream.shape[0]
        wide = projection.shape[1]
        place = lax.axis_index("dp")
        span, core = place // 2, place % 2
        seat = lax.axis_index("tensor")
        scaling = HD ** (-0.5)

        allowed = sequence_mask(lengths[0], rows)
        scores = dot(query, keys, ((1,), (1,))) * scaling
        scores = jnp.where(allowed, scores, -1e30)
        exponent = jnp.exp(scores - jnp.max(scores, axis=1, keepdims=True))
        probs = exponent / jnp.sum(exponent, axis=1, keepdims=True)
        probs_low = probs.astype(bf)
        attended = dot(probs_low, values, ((1,), (0,))).astype(bf)

        pieces = []
        for r in range(tensor):
            piece = lax.dynamic_slice_in_dim(attended, ((seat + r) % tensor) * part, part, 0)
            pieces.append(ring_shift(piece, r) if r else piece)
        mine = jnp.concatenate(pieces, axis=1)
        over = jnp.concatenate([mine] + [span_shift(mine, j) for j in range(1, spans)], axis=0)
        attended_all = jnp.concatenate([over, core_swap(over)], axis=0)

        plus, minus = [projection], [projection]
        for k in range(1, tensor):
            plus.append(up(plus[-1], k - 1, tensor - 1))
            minus.append(down(minus[-1], 1, tensor - k + 1))
        blocks = [projection] + [minus[r] + plus[tensor - r] for r in range(1, tensor)]
        full = jnp.concatenate(blocks, axis=0)

        step = wide // CHUNKS
        split = upstream.reshape(part, spans, 2, wide)
        out_total = 0.0
        finals = []
        for c in range(CHUNKS):
            own, peer = [], []
            for j in range(spans):
                block = lax.dynamic_slice(
                    split[:, :, :, c * step : (c + 1) * step],
                    (0, (span + j) % spans, 0, 0),
                    (part, 1, 2, step),
                )[:, 0]
                block = span_shift(block, j) if j else block
                own.append(lax.dynamic_index_in_dim(block, core, 1, keepdims=False))
                peer.append(core_swap(lax.dynamic_index_in_dim(block, 1 - core, 1, keepdims=False)))
            held = jnp.concatenate(own + peer, axis=0)
            out_total = out_total + dot(held, full[:, c * step : (c + 1) * step], ((1,), (1,)))
            terms = dot(attended_all, held, ((0,), (0,)))
            terms_low = terms.astype(bf)

            def term(r):
                at = (tensor - r) % tensor
                return terms_low[at * HD : (at + 1) * HD]

            rise, fall = None, None
            for j in range(1, tensor):
                a, b = term(tensor - j), term(j)
                rise = up(a if rise is None else a + rise, 0, j)
                fall = down(b if fall is None else b + fall, tensor - j, tensor)
            finals.append(terms[:HD] + rise.astype(jnp.float32) + fall.astype(jnp.float32))
        grad_projection = jnp.concatenate(finals, axis=1)

        half = spans * part
        summed = out_total[:half] + core_swap(out_total[half:].astype(bf)).astype(jnp.float32)
        own_rows = summed[:part]
        for j in range(1, spans):
            own_rows = own_rows + span_shift(summed[j * part : (j + 1) * part].astype(bf), -j).astype(jnp.float32)
        own_rows = own_rows.astype(bf)
        got = [own_rows[:, :HD]] + [ring_shift(own_rows[:, r * HD : (r + 1) * HD], r) for r in range(1, tensor)]
        turned = [got[(tensor - m) % tensor] for m in range(tensor)]
        twice = jnp.concatenate(turned + turned, axis=0)
        out_grad = lax.dynamic_slice_in_dim(twice, (tensor - seat) * part, rows, 0)

        grad_values = dot(probs_low, out_grad, ((0,), (0,))).astype(bf)
        grad_probs = dot(out_grad, values, ((1,), (1,)))
        delta = jnp.sum(probs * grad_probs, axis=1, keepdims=True)
        grad_scores = (probs * (grad_probs - delta) * scaling).astype(bf)
        grad_query = dot(grad_scores, keys, ((1,), (0,))).astype(bf)
        grad_keys = dot(grad_scores, query, ((0,), (0,))).astype(bf)
        return grad_query, grad_keys, grad_values, grad_projection

    return shards


def solution(mesh):
    in_specs = (
        P(("groups", "dp"), "tensor"),
        P(("groups", "dp"), "tensor"),
        P(("groups", "dp"), "tensor"),
        P(("groups", "dp", "tensor"), None),
        P("tensor", "dp"),
        P(("groups", "dp"), None),
    )
    out_specs = (
        P(("groups", "dp"), "tensor"),
        P(("groups", "dp"), "tensor"),
        P(("groups", "dp"), "tensor"),
        P(("groups", "tensor"), "dp"),
    )
    shards = build(mesh.shape["dp"], mesh.shape["tensor"])
    return jax.shard_map(shards, mesh=mesh, in_specs=in_specs, out_specs=out_specs, check_vma=False)
```

```python
import math

import jax
import jax.numpy as jnp
from jax import lax
from jax.experimental import pallas as pl
from jax.experimental.pallas import tpu as pltpu
from jax.sharding import PartitionSpec as P


HD = 128
CUTS = (0, 2, 3, 4)
TILE = 512


def dot(a, b, contract):
    return lax.dot_general(a, b, ((contract[0], contract[1]), ((), ())), preferred_element_type=jnp.float32)


def build(groups, dp, tensor):
    spans = dp // 2
    bf = jnp.bfloat16
    f32 = jnp.float32
    shared = groups == 2

    def send(value, step, cross):
        perm = [(i, ((i // 2 + step) % spans) * 2 + (i % 2 ^ cross)) for i in range(dp)]
        return lax.ppermute(value, "dp", perm)

    def meet(value, r):
        return lax.ppermute(value, "tensor", [(i, i ^ r) for i in range(tensor)])

    def twin(value):
        return lax.ppermute(value, "groups", [(0, 1), (1, 0)])

    vmem = pl.BlockSpec(memory_space=pltpu.VMEM)
    smem = pl.BlockSpec(memory_space=pltpu.SMEM)
    anywhere = pl.BlockSpec(memory_space=pl.ANY)

    def call(kernel, flops, given, specs, shapes, scratch=(), outs=None, aliases=None):
        moved = sum(x.size * x.dtype.itemsize for x in given if x.size < 1 << 20)
        return pl.pallas_call(
            kernel,
            in_specs=specs,
            out_specs=outs or [vmem] * len(shapes),
            out_shape=[jax.ShapeDtypeStruct(s, t) for s, t in shapes],
            scratch_shapes=list(scratch),
            input_output_aliases=aliases or {},
            cost_estimate=pl.CostEstimate(flops=flops, bytes_accessed=moved, transcendentals=0),
        )(*given)

    def cut_call(upstream, projection, columns, width_of):
        part, given = upstream.shape[0], (upstream,)
        shapes = [(part, w) for w in width_of]
        if projection is not None:
            given += (projection,)
            shapes.append((projection.shape[0] // 2, projection.shape[1]))
        count = len(shapes)

        def kernel(*refs):
            outs, held = refs[len(given) : len(given) + count], refs[len(given) + count : len(given) + 2 * count]
            into, out_of = refs[-2:]
            place = lax.axis_index("dp")
            sources = [refs[0].at[:, pl.ds(pl.multiple_of(f(place), 128), w)] for f, w in zip(columns, width_of)]
            if projection is not None:
                rows = shapes[-1][0]
                sources.append(refs[1].at[pl.ds(pl.multiple_of(lax.axis_index("groups") * rows, rows), rows)])
            loads = [pltpu.make_async_copy(x, held[i], into.at[i]) for i, x in enumerate(sources)]
            stores = [pltpu.make_async_copy(held[i], outs[i], out_of.at[i]) for i in range(count)]
            for load in loads:
                load.start()
            for load, store in zip(loads, stores):
                load.wait()
                store.start()
            for store in stores:
                store.wait()

        return call(
            kernel,
            0,
            given,
            [anywhere] * len(given),
            [(shape, bf) for shape in shapes],
            [pltpu.VMEM(shape, bf) for shape in shapes] + [pltpu.SemaphoreType.DMA((count,))] * 2,
            [anywhere] * count,
        )

    def forward_kernel(lengths_ref, query_ref, keys_ref, values_ref, probs_ref, turned_ref):
        rows = query_ref.shape[0]
        part = turned_ref.shape[2]
        down = lax.broadcasted_iota(jnp.int32, (rows, 1), 0)
        across = lax.broadcasted_iota(jnp.int32, (1, rows), 1)
        label_down, label_across = jnp.zeros_like(down), jnp.zeros_like(across)
        end = jnp.int32(0)
        for c in range(lengths_ref.shape[1]):
            end = end + lengths_ref[0, c]
            label_down += (down >= end).astype(jnp.int32)
            label_across += (across >= end).astype(jnp.int32)
        allowed = jnp.logical_and(label_down == label_across, across <= down)
        scores = dot(query_ref[...], keys_ref[...], ((1,), (1,))) * (HD ** (-0.5))
        scores = jnp.where(allowed, scores, -1e30)
        exponent = jnp.exp(scores - jnp.max(scores, axis=1, keepdims=True))
        probs = exponent / jnp.sum(exponent, axis=1, keepdims=True)
        probs_ref[...] = probs
        if part % 128 == 0:
            turned = dot(values_ref[...], probs.astype(bf), ((0,), (1,))).astype(bf)
            for r in range(tensor):
                turned_ref[r] = turned[:, r * part : (r + 1) * part]
        else:
            attended = dot(probs.astype(bf), values_ref[...], ((1,), (0,)))
            for r in range(tensor):
                turned_ref[r] = jnp.transpose(attended[r * part : (r + 1) * part]).astype(bf)

    def forward_call(lengths, query, keys, values, part):
        rows = query.shape[0]
        return call(
            forward_kernel,
            4 * rows * rows * HD,
            (lengths, query, keys, values),
            [smem] + [vmem] * 3,
            [((rows, rows), f32), ((tensor, HD, part), bf)],
        )

    def backward_kernel(
        probs_ref, query_ref, keys_ref, values_ref, out_grad_ref, grad_query_ref, grad_keys_ref, grad_values_ref
    ):
        out_grad = out_grad_ref[...]
        probs = probs_ref[...]
        grad_probs = dot(out_grad, values_ref[...], ((1,), (1,)))
        delta = jnp.sum(probs * grad_probs, axis=1, keepdims=True)
        grad_scores = (probs * (grad_probs - delta) * (HD ** (-0.5))).astype(bf)
        grad_query_ref[...] = dot(grad_scores, keys_ref[...], ((1,), (0,))).astype(bf)
        grad_keys_ref[...] = dot(grad_scores, query_ref[...], ((0,), (0,))).astype(bf)
        grad_values_ref[...] = dot(probs.astype(bf), out_grad, ((0,), (0,))).astype(bf)

    def whole(shape):
        return pl.BlockSpec(shape, lambda *_: (0, 0))

    def terms_kernel(index_ref, *refs):
        seat = lax.axis_index("tensor")
        blocks = []
        for r in [2 * n for n in range(tensor // 2)] + [2 * n + 1 for n in range(tensor // 2)]:
            at = pl.ds(pl.multiple_of((seat ^ r) * HD, HD), HD)
            blocks.append(jnp.concatenate([a[at, :] for a in refs[:dp]], axis=1))
        attended = jnp.concatenate(blocks, axis=0)
        first, swapped, *rest = refs[dp : 2 * dp]
        held = [first] + rest[: spans - 1] + [swapped] + rest[spans - 1 :]
        held = jnp.concatenate([p[...] for p in held], axis=0)
        kept_ref, low_ref, sent_ref = refs[2 * dp :]
        terms = dot(attended, held, ((1,), (0,)))
        kept_ref[...] = terms[:HD]
        half = tensor // 2 * HD
        if tensor > 2:
            low_ref[...] = terms[HD:half].astype(bf)
        sent_ref[...] = terms[half:].astype(bf)

    def terms_call(place, attended, upstream, swapped, pieces, start):
        part, step = pieces[0].shape
        wide = swapped.shape[1]
        size = math.gcd(math.gcd(step, start), TILE) if start else math.gcd(step, TILE)
        tiles = step // size
        shapes = [((HD, step), f32), ((max(1, tensor // 2 - 1) * HD, step), bf), ((tensor // 2 * HD, step), bf)]
        tile = lambda shape: pl.BlockSpec((shape[0], size), lambda i, *_: (0, i))
        index = jnp.full((1,), (place * wide + start) // size, jnp.int32)
        return pl.pallas_call(
            terms_kernel,
            grid_spec=pltpu.PrefetchScalarGridSpec(
                num_scalar_prefetch=1,
                grid=(tiles,),
                in_specs=[whole(a.shape) for a in attended]
                + [pl.BlockSpec((part, size), lambda i, s: (0, s[0] + i))]
                + [pl.BlockSpec((part, size), lambda i, s: (0, start // size + i))]
                + [tile(p.shape) for p in pieces],
                out_specs=[tile(s) for s, _ in shapes],
            ),
            out_shape=[jax.ShapeDtypeStruct(s, t) for s, t in shapes],
            cost_estimate=pl.CostEstimate(
                flops=2 * dp * part * tensor * HD * step,
                bytes_accessed=2 * (dp * part * tensor * HD + dp * part * step + tensor * HD * step),
                transcendentals=0,
            ),
            name="terms",
        )(index, *attended, upstream, swapped, *pieces)

    def out_kernel(count, index_ref, upstream_ref, swapped_ref, base_ref, *refs):
        many = (tensor - 1) * (2 if shared else 1)
        blocks, pieces, (kept_ref, sent_ref, full) = refs[:many], refs[many:-3], refs[-3:]
        part = upstream_ref.shape[0]
        seat = lax.axis_index("tensor")
        full[pl.ds(pl.multiple_of(seat * HD, HD), HD)] = base_ref[...]
        for r in range(1, tensor):
            at = (seat ^ r) * HD
            if shared:
                half = HD // 2
                mine = lax.axis_index("groups") * half
                full[pl.ds(pl.multiple_of(at + mine, half), half)] = blocks[2 * r - 2][...]
                full[pl.ds(pl.multiple_of(at + half - mine, half), half)] = blocks[2 * r - 1][...]
            else:
                full[pl.ds(pl.multiple_of(at, HD), HD)] = blocks[r - 1][...]
        rows = [jnp.concatenate([pieces[c * (dp - 2) + p][...] for c in range(count)], axis=1) for p in range(dp - 2)]
        rows = [upstream_ref[...]] + rows[: spans - 1] + [swapped_ref[...]] + rows[spans - 1 :]
        total = dot(jnp.concatenate(rows, axis=0), full[...], ((1,), (1,)))
        half = spans * part
        kept_ref[...] = total[:half]
        sent_ref[...] = total[half:].astype(bf)

    def out_call(index, upstream, swapped, projection, blocks, pieces):
        part, wide, count = upstream.shape[0], projection.shape[1], len(pieces)
        flat = [p for row in pieces for p in row]
        shape = (spans * part, tensor * HD)
        return pl.pallas_call(
            lambda *refs: out_kernel(count, *refs),
            grid_spec=pltpu.PrefetchScalarGridSpec(
                num_scalar_prefetch=1,
                grid=(1,),
                in_specs=[pl.BlockSpec((part, wide), lambda i, s: (0, s[0]))]
                + [whole(p.shape) for p in [swapped, projection] + blocks + flat],
                out_specs=[whole(shape)] * 2,
                scratch_shapes=[pltpu.VMEM((tensor * HD, wide), bf)],
            ),
            out_shape=[jax.ShapeDtypeStruct(shape, f32), jax.ShapeDtypeStruct(shape, bf)],
            cost_estimate=pl.CostEstimate(
                flops=4 * shape[0] * shape[1] * wide,
                bytes_accessed=2 * (dp * part * wide + tensor * projection.size + 3 * shape[0] * shape[1]),
                transcendentals=0,
            ),
            name="outs",
        )(index, upstream, swapped, projection, *blocks, *flat)

    def shards(query, keys, values, upstream, projection, lengths):
        rows = query.shape[0]
        part = upstream.shape[0]
        wide = projection.shape[1]
        place = lax.axis_index("dp")
        bounds = [wide * cut // CUTS[-1] for cut in CUTS]
        chunks = list(zip(bounds, bounds[1:]))
        ways = [(j, 0) for j in range(1, spans)] + [(j, 1) for j in range(1, spans)]

        def cut(source, parts, extra, swap):
            columns, widths = [], []
            for c in parts:
                for j, cross in ways:
                    start, stop = chunks[c]
                    columns.append(lambda p, j=j, cross=cross, start=start: target(p, j, cross) * wide + start)
                    widths.append(stop - start)
            if swap:
                columns.append(lambda p: target(p, 0, 1) * wide)
                widths.append(wide)
            return cut_call(source, extra, columns, widths)

        def target(p, j, cross):
            return ((p // 2 + j) % spans) * 2 + ((p % 2) ^ cross)

        def spread(pieces):
            return [send(x, j, cross) for x, (j, cross) in zip(pieces, ways)]

        first = cut(upstream, [0], projection if shared else None, False)
        held = [spread(first)]

        probs, turned = forward_call(lengths, query, keys, values, part)
        mine = lax.all_to_all(turned, "tensor", 0, 0, tiled=True).reshape(tensor * HD, part)
        over = [mine] + [send(mine, j, 0) for j in range(1, spans)]
        attended = over + [send(piece, 0, 1) for piece in over]

        later, _ = lax.optimization_barrier((upstream, turned))
        rest = cut(later, range(1, len(chunks)), None, True)
        for c in range(1, len(chunks)):
            held.append(spread(rest[(c - 1) * len(ways) :]))
        swapped = send(rest[-1], 0, 1)

        half = first[-1] if shared else projection
        known = {0: half}
        bit = tensor // 2
        while bit:
            known.update({r ^ bit: meet(block, bit) for r, block in sorted(known.items())})
            bit //= 2
        blocks = []
        for r in range(1, tensor):
            blocks += [known[r], twin(known[r])] if shared else [known[r]]

        grad_projection = None
        for c, (start, stop) in enumerate(chunks):
            step = stop - start
            kept, low, sent = terms_call(place, attended, upstream, swapped, held[c], start)
            near = meet(sent, 1)
            rest = []
            for n in range(1, tensor // 2):
                rest.append(low[(n - 1) * HD : n * HD] + near[n * HD : (n + 1) * HD])
            rest = dict(enumerate(rest, 1))
            far, bit = [], 1
            while rest:
                going = [n for n in sorted(rest) if n & bit]
                bundle = rest[going[0]] if len(going) == 1 else jnp.concatenate([rest[n] for n in going], axis=0)
                came = meet(bundle, 2 * bit)
                rest = {n: v for n, v in rest.items() if not n & bit}
                for i, n in enumerate(going):
                    piece = came[i * HD : (i + 1) * HD] if len(going) > 1 else came
                    if n == bit:
                        far.append(piece)
                    else:
                        rest[n ^ bit] = rest[n ^ bit] + piece
                bit *= 2
            total = kept + near[:HD].astype(f32)
            for piece in far:
                total = total + piece.astype(f32)
            if grad_projection is None:
                grad_projection = jnp.pad(total, ((0, 0), (0, wide - step)))
            else:
                grad_projection = lax.dynamic_update_slice(grad_projection, total, (0, start))

        kept, sent = out_call(jnp.full((1,), place, jnp.int32), upstream, swapped, projection, blocks, held)
        summed = kept + send(sent, 0, 1).astype(f32)
        own_rows = summed[:part]
        for j in range(1, spans):
            own_rows = own_rows + send(summed[j * part : (j + 1) * part].astype(bf), -j, 0).astype(f32)
        own_rows = own_rows.astype(bf)
        pieces = jnp.transpose(own_rows.reshape(part, tensor, HD), (1, 0, 2))
        out_grad = lax.all_to_all(pieces, "tensor", 0, 0, tiled=True).reshape(rows, HD)

        grads = call(
            backward_kernel,
            10 * rows * rows * HD,
            (probs, query, keys, values, out_grad),
            [vmem] * 5,
            [((rows, HD), bf)] * 3,
        )
        return (*grads, grad_projection)

    return shards


def solution(mesh):
    in_specs = (
        P(("groups", "dp"), "tensor"),
        P(("groups", "dp"), "tensor"),
        P(("groups", "dp"), "tensor"),
        P(("groups", "dp", "tensor"), None),
        P("tensor", "dp"),
        P(("groups", "dp"), None),
    )
    out_specs = (
        P(("groups", "dp"), "tensor"),
        P(("groups", "dp"), "tensor"),
        P(("groups", "dp"), "tensor"),
        P(("groups", "tensor"), "dp"),
    )
    shards = build(mesh.shape["groups"], mesh.shape["dp"], mesh.shape["tensor"])

    return jax.shard_map(shards, mesh=mesh, in_specs=in_specs, out_specs=out_specs, check_vma=False)
```
